32 devices in a mesh: row: 4 (over z), col: 8 (over y, x, core).
Axes of the slice: x: 2, y: 2, z: 4, core: 2. Of those that a mesh axis runs over, the one named last changes fastest.
Arguments:
- hessian: float32 [18432, 18432], P('row', 'col'), may hold values from -1 to 5, as said below
- right_side: float32 [18432, 512], P('row'), may hold values from -6 to 6
- mask: int32 [18432, 512], P('row'), may hold values 0 or 1
- damping: float32 [1], replicated, may hold values from 0.4 to 1.2
Outputs:
- solution: float32 [18432, 512], P('row')
The draws below stay inside these ranges and needn't reach their ends.
Inputs may be any that keep to these rules, and one draw needn't show every extreme that they name: hessian is symmetric and positive definite.
All inputs are finite; a program needn't handle non-finite values. No bound on the sum of `mask` on one device may be relied on, other than what follows from the above.
Results may differ from the reference program's by a relative error of at most 0.0001.
Values sent between devices are 32-bit elements; how exact they have to be, the bound alone decides.
No kernel may reach another device: no remote copies, remote signals or barrier semaphores. Data moves between devices by JAX's collectives and lax.ppermute only.
A program may use at most 192 MiB of HBM per device.

```python
import math
import jax
import jax.numpy as jnp
from jax import lax

ORDER = 18432
COLS = 512
ITERS = 3


def draw_hessian(key, part):
    key_noise, key_diagonal = jax.random.split(jax.random.fold_in(key, 11))
    spread = 0.5 / math.sqrt(ORDER)
    noise_field = jax.random.normal(key_noise, (ORDER, ORDER), jnp.float32)
    symmetric = (noise_field + noise_field.T) * (spread * 0.70710678)
    diagonal = jnp.exp(jax.random.uniform(key_diagonal, (ORDER,), jnp.float32, math.log(0.8), math.log(5.0)))
    positions = jnp.arange(ORDER)
    return symmetric.at[positions, positions].set(diagonal)


def place_ends(drawn, key, low, top_value):
    place = [jax.random.randint(jax.random.fold_in(key, axis), (), 0, length) for axis, length in enumerate(drawn.shape)]
    main_axis = drawn.shape.index(max(drawn.shape))
    next_to = place[:main_axis] + [(place[main_axis] + 1) % drawn.shape[main_axis]] + place[main_axis + 1:]
    return drawn.at[tuple(place)].set(low).at[tuple(next_to)].set(top_value)


def level_of(rng, shape, pieces, least, top_value):
    def one(axis_at, blocks):
        draws = jax.random.uniform(jax.random.fold_in(jax.random.fold_in(rng, 6), axis_at), (blocks,), jnp.float32, least / len(pieces), top_value / len(pieces))
        return jnp.repeat(jnp.exp(draws), shape[axis_at] // blocks).reshape((-1,) + (1,) * (len(shape) - axis_at - 1))

    level = one(*pieces[0])
    for cut in pieces[1:]:
        level = level * one(*cut)
    return level


def bell_draw(stream_key, shape, deviation, most, cuts=(), held_as=jnp.bfloat16):
    values = jax.random.normal(stream_key, shape, jnp.float32) * deviation
    if len(cuts) > 0:
        values = level_of(stream_key, shape, cuts, -0.22, 0.18) * values
    return jnp.clip(values, min=-most, max=most).astype(held_as)


def setup_inputs(seed: int = 0) -> dict:
    key_list = jax.random.split(jax.random.key(seed), 5)
    return {
        "hessian": draw_hessian(jax.random.fold_in(key_list[4], 71), 0),
        "right_side": bell_draw(key_list[1], (ORDER, COLS), 1.0, 6.0, ((0, 4),), jnp.float32),
        "mask": place_ends((jax.random.randint(key_list[2], (ORDER, COLS), 0, 4) < 3).astype(jnp.int32), jax.random.fold_in(key_list[2], 1), 0, 1),
        "damping": jnp.clip(jnp.exp(jax.random.uniform(key_list[3], (1,), jnp.float32, math.log(0.4), math.log(1.2))), 0.4, 1.2),
    }


epsilon = 1e-6


def reference(hessian, right_side, mask, damping):
    mask_float = mask.astype(jnp.float32)
    damping_value = damping[0]

    def masked_apply(vector):
        product = jnp.dot(hessian, vector, precision=lax.Precision.HIGHEST, preferred_element_type=jnp.float32)
        return mask_float * (product + damping_value * vector)

    residual = mask_float * right_side
    direction = residual
    solution = jnp.zeros_like(right_side)
    norm_now = jnp.sum(residual * residual, axis=0)
    for iteration in range(ITERS):
        applied = masked_apply(direction)
        curvature = jnp.sum(direction * applied, axis=0)
        step_size = norm_now / (curvature + epsilon)
        solution = solution + step_size * direction
        residual = residual - step_size * applied
        norm_next = jnp.sum(residual * residual, axis=0)
        direction = residual + (norm_next / (norm_now + epsilon)) * direction
        norm_now = norm_next
    return solution
```

```python
import functools

import jax
import jax.numpy as jnp
from jax import lax
from jax.experimental import pallas as pl
from jax.experimental.pallas import tpu as pltpu
from jax.sharding import PartitionSpec as P

CHUNKS = 2
epsilon = 1e-06
F32, BF16 = jnp.float32, jnp.bfloat16
VMEM_LIMIT = 48 << 20


def split(value):
    high = value.astype(BF16)
    return high, (value - high.astype(F32)).astype(BF16)


def down(left, right):
    return lax.dot_general(
        left, right, (((0,), (0,)), ((), ())), preferred_element_type=F32
    )


def product_kernel(layout, place_ref, h_ref, *refs):
    n_piece, ratio, piece, sub, low_terms, fresh = layout
    n_in = 2 if fresh else ratio
    inputs, outputs = refs[:n_in], refs[n_in : n_in + n_piece]
    x_out = None if fresh else refs[n_in + n_piece]
    terms, sums = refs[-2], refs[-1]
    step = pl.program_id(0)
    rows, width = h_ref.shape
    columns = sums.shape[1]
    block = n_piece * piece

    def keep(value, at):
        high, low = split(value)
        terms[at, :columns] = high
        if low_terms:
            terms[at, columns:] = low

    @pl.when(step == 0)
    def _():
        if fresh:
            right_ref, mask_ref = inputs

            def body(s, carry):
                at = pl.ds(pl.multiple_of(s * piece, 16), piece)
                keep(mask_ref[at, :].astype(F32) * right_ref[at, :], at)
                return carry

            lax.fori_loop(0, rows // piece, body, 0)
        else:
            for j in range(ratio):
                for k in range(n_piece):
                    base = (place_ref[1] ^ j) * block + (place_ref[0] ^ k) * piece
                    at = pl.ds(pl.multiple_of(base, 16), piece)
                    value = inputs[j][k * piece : (k + 1) * piece, :]
                    keep(value, at)
                    x_out[at, :] = value

    summed = None
    for s in range(rows // sub):
        at = slice(s * sub, (s + 1) * sub)
        high, low = split(h_ref[at, :])
        part = down(high, terms[at, :])
        if low_terms:
            part = part[:, :columns] + part[:, columns:]
        part = part + down(low, terms[at, :columns])
        summed = part if summed is None else summed + part
    sums[pl.ds(pl.multiple_of(step * width, 128), width), :] = summed

    @pl.when(step == pl.num_programs(0) - 1)
    def _():
        for k in range(n_piece):
            at = pl.ds(pl.multiple_of((place_ref[0] ^ k) * piece, 16), piece)
            outputs[k][...] = sums[at, :]


def product(hessian, place, inputs, columns, piece, chunk=None, low_terms=True):
    rows, block = hessian.shape
    n_piece = block // piece
    ratio = rows // block
    fresh = chunk is not None
    width = max(w for w in (128, 256, 384) if block % w == 0 and w * rows <= 1 << 21)
    sub = min(rows, 2304)
    if rows % sub:
        sub = rows
    whole = lambda shape, at=0: pl.BlockSpec(shape, lambda i, p: (0, at))
    if fresh:
        in_specs = [whole((rows, columns), chunk)] * 2
    else:
        in_specs = [whole((block, columns))] * ratio
    out_shape = [jax.ShapeDtypeStruct((piece, columns), F32)] * n_piece
    out_specs = [whole((piece, columns))] * n_piece
    if not fresh:
        out_shape.append(jax.ShapeDtypeStruct((rows, columns), F32))
        out_specs.append(whole((rows, columns)))
    layout = (n_piece, ratio, piece, sub, low_terms, fresh)
    passes = 3 if low_terms else 2
    return pl.pallas_call(
        functools.partial(product_kernel, layout),
        out_shape=out_shape,
        grid_spec=pltpu.PrefetchScalarGridSpec(
            num_scalar_prefetch=1,
            grid=(block // width,),
            in_specs=[pl.BlockSpec((rows, width), lambda i, p: (0, i))] + in_specs,
            out_specs=out_specs,
            scratch_shapes=[
                pltpu.VMEM((rows, columns * (2 if low_terms else 1)), BF16),
                pltpu.VMEM((block, columns), F32),
            ],
        ),
        compiler_params=pltpu.CompilerParams(
            dimension_semantics=("arbitrary",), vmem_limit_bytes=VMEM_LIMIT
        ),
        cost_estimate=pl.CostEstimate(
            flops=2 * passes * rows * block * columns,
            bytes_accessed=4 * (rows * block + rows * columns + block * columns),
            transcendentals=0,
        ),
    )(place, hessian, *inputs)


def assemble_kernel(place_ref, *refs):
    pieces, out_ref = refs[:-1], refs[-1]
    size = pieces[0].shape[0]
    for k, piece in enumerate(pieces):
        at = pl.ds(pl.multiple_of((place_ref[0] ^ k) * size, 8), size)
        out_ref[at, :] = piece[...]


def assemble(pieces, place):
    size, columns = pieces[0].shape
    return pl.pallas_call(
        assemble_kernel,
        out_shape=jax.ShapeDtypeStruct((size * len(pieces), columns), F32),
        in_specs=[pl.BlockSpec(memory_space=pltpu.SMEM)]
        + [pl.BlockSpec(memory_space=pltpu.VMEM)] * len(pieces),
        out_specs=pl.BlockSpec(memory_space=pltpu.VMEM),
        cost_estimate=pl.CostEstimate(
            flops=0,
            bytes_accessed=8 * size * columns * len(pieces),
            transcendentals=0,
        ),
    )(place, *pieces)


def swap(block, axis, distance):
    size = lax.axis_size(axis)
    return lax.ppermute(block, axis, [(i, i ^ distance) for i in range(size)])


def total(parts):
    parts = jnp.stack(parts)
    for axis in ("col", "row"):
        distance = 1
        while distance < lax.axis_size(axis):
            parts = parts + swap(parts, axis, distance)
            distance *= 2
    return parts


def column_dot(first, second):
    return jnp.sum(first * second, axis=0)


def take(whole, place, size):
    return lax.dynamic_slice_in_dim(whole, place, size, 0)


def on_device(hessian, right_side, mask, damping):
    n_row, n_col = lax.axis_size("row"), lax.axis_size("col")
    ratio = n_col // n_row
    rows, block = hessian.shape
    piece = rows // n_col
    columns = right_side.shape[1] // CHUNKS
    damping_value = damping[0]
    col = lax.axis_index("col")
    plane, half = col // ratio, col % ratio
    level = lax.axis_index("row")
    own_place = half * block + plane * piece
    at_plane = jnp.stack([plane, half]).astype(jnp.int32)
    at_level = jnp.stack([level]).astype(jnp.int32)

    def to_home(pieces):
        got = [pieces[0]] + [swap(pieces[k], "col", k * ratio) for k in range(1, n_row)]
        blocks = assemble(got, at_plane)
        return lax.psum_scatter(blocks, "row", scatter_dimension=0, tiled=True)

    def to_plane(shard):
        got = [shard] + [swap(shard, "col", k * ratio) for k in range(1, n_row)]
        mine = jnp.concatenate(got, axis=0)
        return [mine] + [swap(mine, "col", k) for k in range(1, ratio)]

    def turned(shard):
        levels = assemble(
            [shard] + [swap(shard, "row", k) for k in range(1, n_row)], at_level
        )
        got = [take(levels, plane * piece, piece)]
        for k in range(1, n_row):
            got.append(swap(take(levels, (plane ^ k) * piece, piece), "col", k * ratio))
        return got

    def masked(mask_own, summed, own):
        return mask_own * (summed + damping_value * own)

    chunks, first = [], []
    for chunk in range(CHUNKS):
        cut = slice(chunk * columns, (chunk + 1) * columns)
        mask_own = take(mask[:, cut], own_place, piece).astype(F32)
        r0_own = mask_own * take(right_side[:, cut], own_place, piece)
        pieces = product(
            hessian, at_plane, (right_side, mask), columns, piece, chunk=chunk
        )
        u_own = masked(mask_own, to_home(pieces), r0_own)
        chunks.append((mask_own, r0_own))
        first.append(u_own)
    scalars = total(
        [
            jnp.concatenate([column_dot(c[1], f) for c, f in zip(chunks, others)])
            for others in ([c[1] for c in chunks], first)
        ]
    )

    outputs = []
    for chunk in range(CHUNKS):
        cut = slice(chunk * columns, (chunk + 1) * columns)
        (mask_own, r0_own), u_own = chunks[chunk], first[chunk]
        n0, c00 = scalars[:, cut]
        *pieces, u = product(hessian, at_plane, to_plane(u_own), columns, piece)
        uu_own = masked(mask_own, to_home(pieces), u_own)
        a0 = n0 / (c00 + epsilon)
        r1_own = r0_own - a0 * u_own
        s1_own = u_own - a0 * uu_own
        n1, c11, c01, c10 = total(
            [
                column_dot(r1_own, r1_own),
                column_dot(r1_own, s1_own),
                column_dot(r0_own, s1_own),
                column_dot(r1_own, u_own),
            ]
        )
        b0 = n1 / (n0 + epsilon)
        curve1 = c11 + b0 * (c01 + c10) + b0 * b0 * c00
        a1 = n1 / (curve1 + epsilon)
        t1_own = s1_own + b0 * u_own
        r2_own = r1_own - a1 * t1_own
        *pieces, r2 = product(
            hessian, at_plane, to_plane(r2_own), columns, piece, low_terms=False
        )
        form = 0.0
        for p, x in zip(pieces, turned(r2_own)):
            form += column_dot(p, 2.0 * x - lax.reduce_precision(x, 8, 7))
        form, n2, cross = total(
            [form, column_dot(r2_own, r2_own), column_dot(r2_own, t1_own)]
        )
        b1 = n2 / (n1 + epsilon)
        curve2 = form + damping_value * n2 + 2.0 * b1 * cross + b1 * b1 * curve1
        a2 = n2 / (curve2 + epsilon)
        r0 = mask[:, cut].astype(F32) * right_side[:, cut]
        d1 = (1.0 + b0) * r0 - a0 * u
        outputs.append(a0 * r0 + (a1 + a2 * b1) * d1 + a2 * r2)
    return jnp.concatenate(outputs, axis=1)


def solution(mesh):
    in_specs = (P("row", "col"), P("row", None), P("row", None), P())
    out_specs = P("row", None)
    return jax.shard_map(
        on_device, mesh=mesh, in_specs=in_specs, out_specs=out_specs, check_vma=False
    )
```

```python
import functools

import jax
import jax.numpy as jnp
from jax import lax
from jax.experimental import pallas as pl
from jax.experimental.pallas import tpu as pltpu
from jax.sharding import PartitionSpec as P


CHUNKS = 2
epsilon = 1e-06
F32, BF16 = jnp.float32, jnp.bfloat16
VMEM_LIMIT = 48 << 20


def strip_of(size):
    return next(s for s in (64, 48, 32, 16) if size % s == 0)


def split(value):
    high = value.astype(BF16)
    return high, (value - high.astype(F32)).astype(BF16)


def down(left, right):
    return lax.dot_general(
        left, right, (((0,), (0,)), ((), ())), preferred_element_type=F32
    )


def copy_strips(source, source_base, target, target_base, size):
    strip = strip_of(size)

    def body(s, carry):
        here = pl.ds(pl.multiple_of(source_base + s * strip, 16), strip)
        there = pl.ds(pl.multiple_of(target_base + s * strip, 16), strip)
        target[there, :] = source[here, :]
        return carry

    lax.fori_loop(0, size // strip, body, 0)


def product_kernel(layout, place_ref, h_ref, *refs):
    n_piece, ratio, piece, sub, low_terms, fresh, n_after = layout
    n_in = 2 if fresh else ratio
    inputs, refs = refs[:n_in], refs[n_in + n_after :]
    outputs = refs[:n_piece]
    x_out = None if fresh else refs[n_piece]
    terms, sums = refs[-2], refs[-1]
    step = pl.program_id(0)
    rows, width = h_ref.shape
    columns = sums.shape[1]
    block = n_piece * piece
    strip = strip_of(piece)

    def keep(value, at):
        high, low = split(value)
        terms[at, :columns] = high
        if low_terms:
            terms[at, columns:] = low

    @pl.when(step == 0)
    def _():
        if fresh:
            right_ref, mask_ref = inputs

            def body(s, carry):
                at = pl.ds(pl.multiple_of(s * strip, strip), strip)
                keep(mask_ref[at, :].astype(F32) * right_ref[at, :], at)
                return carry

            lax.fori_loop(0, rows // strip, body, 0)
        else:
            for j in range(ratio):
                for k in range(n_piece):
                    base = (place_ref[1] ^ j) * block + (place_ref[0] ^ k) * piece

                    def body(s, carry, j=j, k=k, base=base):
                        start = pl.multiple_of(k * piece + s * strip, strip)
                        at = pl.ds(pl.multiple_of(base + s * strip, 16), strip)
                        value = inputs[j][pl.ds(start, strip), :]
                        keep(value, at)
                        x_out[at, :] = value
                        return carry

                    lax.fori_loop(0, piece // strip, body, 0)

    summed = None
    for s in range(rows // sub):
        at = slice(s * sub, (s + 1) * sub)
        high, low = split(h_ref[at, :])
        part = down(high, terms[at, :])
        if low_terms:
            part = part[:, :columns] + part[:, columns:]
        part = part + down(low, terms[at, :columns])
        summed = part if summed is None else summed + part
    sums[pl.ds(pl.multiple_of(step * width, 128), width), :] = summed

    @pl.when(step == pl.num_programs(0) - 1)
    def _():
        for k in range(n_piece):
            copy_strips(sums, (place_ref[0] ^ k) * piece, outputs[k], 0, piece)


def product(hessian, place, inputs, columns, piece, chunk=None, after=()):
    low_terms = True
    rows, block = hessian.shape
    n_piece = block // piece
    ratio = rows // block
    fresh = chunk is not None
    width = max(w for w in (128, 256, 384) if block % w == 0 and w * rows <= 1 << 21)
    sub = min(rows, 2304)
    if rows % sub:
        sub = rows
    whole = lambda shape, at=0: pl.BlockSpec(shape, lambda i, p: (0, at))
    if fresh:
        in_specs = [whole((rows, columns), chunk)] * 2
    else:
        in_specs = [whole((block, columns))] * ratio
    out_shape = [jax.ShapeDtypeStruct((piece, columns), F32)] * n_piece
    out_specs = [whole((piece, columns))] * n_piece
    if not fresh:
        out_shape.append(jax.ShapeDtypeStruct((rows, columns), F32))
        out_specs.append(whole((rows, columns)))
    in_specs += [pl.BlockSpec(memory_space=pl.ANY)] * len(after)
    layout = (n_piece, ratio, piece, sub, low_terms, fresh, len(after))
    passes = 3 if low_terms else 2
    return pl.pallas_call(
        functools.partial(product_kernel, layout),
        out_shape=out_shape,
        grid_spec=pltpu.PrefetchScalarGridSpec(
            num_scalar_prefetch=1,
            grid=(block // width,),
            in_specs=[pl.BlockSpec((rows, width), lambda i, p: (0, i))] + in_specs,
            out_specs=out_specs,
            scratch_shapes=[
                pltpu.VMEM((rows, columns * (2 if low_terms else 1)), BF16),
                pltpu.VMEM((block, columns), F32),
            ],
        ),
        compiler_params=pltpu.CompilerParams(
            dimension_semantics=("arbitrary",), vmem_limit_bytes=VMEM_LIMIT
        ),
        cost_estimate=pl.CostEstimate(
            flops=2 * passes * rows * block * columns,
            bytes_accessed=4 * (rows * block + rows * columns + block * columns),
            transcendentals=0,
        ),
    )(place, hessian, *inputs, *after)


def assemble_kernel(count, place_ref, *refs):
    pieces, out_ref = refs[:count], refs[-1]
    size = pieces[0].shape[0]
    for k, piece in enumerate(pieces):
        copy_strips(piece, 0, out_ref, (place_ref[0] ^ k) * size, size)


def assemble(pieces, place, after=()):
    size, columns = pieces[0].shape
    return pl.pallas_call(
        functools.partial(assemble_kernel, len(pieces)),
        out_shape=jax.ShapeDtypeStruct((size * len(pieces), columns), F32),
        in_specs=[pl.BlockSpec(memory_space=pltpu.SMEM)]
        + [pl.BlockSpec(memory_space=pltpu.VMEM)] * len(pieces)
        + [pl.BlockSpec(memory_space=pl.ANY)] * len(after),
        out_specs=pl.BlockSpec(memory_space=pltpu.VMEM),
        cost_estimate=pl.CostEstimate(
            flops=0,
            bytes_accessed=8 * size * columns * len(pieces),
            transcendentals=0,
        ),
    )(place, *pieces, *after)


def swap(block, axis, distance):
    size = lax.axis_size(axis)
    return lax.ppermute(block, axis, [(i, i ^ distance) for i in range(size)])


def total(parts):
    parts = jnp.stack(parts)
    for axis in ("col", "row"):
        distance = 1
        while distance < lax.axis_size(axis):
            parts = parts + swap(parts, axis, distance)
            distance *= 2
    return parts


def column_dot(first, second):
    return jnp.sum(first * second, axis=0)


def take(whole, place, size):
    return lax.dynamic_slice_in_dim(whole, place, size, 0)


def finish_kernel(coef_ref, right_ref, mask_ref, u_ref, r2_ref, *refs):
    strip = strip_of(u_ref.shape[0])

    def body(s, carry):
        at = pl.ds(pl.multiple_of(s * strip, strip), strip)
        r0 = mask_ref[at, :].astype(F32) * right_ref[at, :]
        value = coef_ref[0] * r0 + coef_ref[1] * u_ref[at, :] + coef_ref[2] * r2_ref[at, :]
        refs[-1][at, :] = value
        return carry

    lax.fori_loop(0, u_ref.shape[0] // strip, body, 0)


def finish(coef, right_side, mask, u, r2, chunk, buffer):
    rows, columns = u.shape
    size = rows // 8
    here = pl.BlockSpec((size, columns), lambda i: (i, chunk))
    own = pl.BlockSpec((size, columns), lambda i: (i, 0))
    given = [] if buffer is None else [buffer]
    return pl.pallas_call(
        finish_kernel,
        out_shape=jax.ShapeDtypeStruct(right_side.shape, F32),
        grid=(8,),
        in_specs=[pl.BlockSpec(coef.shape, lambda i: (0, 0, 0)), here, here, own, own]
        + [pl.BlockSpec(memory_space=pl.ANY)] * len(given),
        out_specs=here,
        input_output_aliases={5: 0} if given else {},
        cost_estimate=pl.CostEstimate(
            flops=6 * rows * columns, bytes_accessed=20 * rows * columns, transcendentals=0
        ),
    )(coef, right_side, mask, u, r2, *given)


def on_device(hessian, right_side, mask, damping):
    n_row, n_col = lax.axis_size("row"), lax.axis_size("col")
    ratio = n_col // n_row
    rows, block = hessian.shape
    piece = rows // n_col
    columns = right_side.shape[1] // CHUNKS
    damping_value = damping[0]
    col = lax.axis_index("col")
    plane, half = col // ratio, col % ratio
    level = lax.axis_index("row")
    own_place = half * block + plane * piece
    at_plane = jnp.stack([plane, half]).astype(jnp.int32)
    at_level = jnp.stack([level]).astype(jnp.int32)
    everyone = range(1, n_row)

    def exchange(pieces):
        return [pieces[0]] + [swap(pieces[k], "col", k * ratio) for k in everyone]

    def place_blocks(pieces, after):
        return assemble(pieces, at_plane, after)

    def home(blocks):
        return lax.psum_scatter(blocks, "row", scatter_dimension=0, tiled=True)

    def to_plane(shard):
        got = exchange([shard] * n_row)
        mine = assemble(got, jnp.zeros_like(at_level))
        return [mine] + [swap(mine, "col", k) for k in range(1, ratio)]

    def turned(shard):
        low, high = jnp.split(shard, 2, axis=1)
        got = [low]
        for k in everyone:
            got.append(swap(jnp.where((level ^ k) < level, low, high), "row", k))
        levels = assemble(got, at_level)
        return levels

    def turned_out(levels, after):
        levels, _ = lax.optimization_barrier((levels, after))
        pieces = [take(levels, (plane ^ k) * piece, piece) for k in range(n_row)]
        return exchange(pieces)

    def form_of(pieces, levels, others, mine):
        levels, pieces = lax.optimization_barrier((levels, pieces))
        others = [take(levels, plane * piece, piece)] + others[1:]
        summed, own = 0.0, 0.0
        for k in range(n_row):
            low, high = jnp.split(pieces[k], 2, axis=1)
            summed += column_dot(jnp.where(plane > level, low, high), others[k])
            own += column_dot(pieces[k], mine[k * piece : (k + 1) * piece])
        zero = jnp.zeros_like(summed)
        pair = jnp.concatenate(
            [
                jnp.where(plane > level, 2.0 * summed, zero),
                jnp.where(plane < level, 2.0 * summed, zero),
            ]
        )
        return jnp.where(plane == level, own, pair)

    def masked(mask_own, summed, own):
        return mask_own * (summed + damping_value * own)

    each = range(CHUNKS)
    cuts = [slice(c * columns, (c + 1) * columns) for c in each]
    mask_all = take(mask, own_place, piece).astype(F32)
    r0_all = mask_all * take(right_side, own_place, piece)
    mask_own = [mask_all[:, cut] for cut in cuts]
    r0_own = [r0_all[:, cut] for cut in cuts]

    def products(inputs, afters, fresh=False):
        pieces, wholes = [], []
        for c in each:
            after = [*afters[c], *(pieces[-1][:1] if c else ())]
            chunk = c if fresh else None
            out = product(hessian, at_plane, inputs[c], columns, piece, chunk, after)
            pieces.append(out[:n_row])
            wholes.extend(out[n_row:])
        return pieces, wholes

    none = [[]] * CHUNKS
    firsts, _ = products([(right_side, mask)] * CHUNKS, none, True)
    got = [exchange(firsts[c]) for c in each]
    blocks = [place_blocks(got[0], firsts[-1][:1])]
    blocks += [place_blocks(got[c], blocks[:1]) for c in each[1:]]
    u_own, gathered = [], []
    for c in each:
        summed = home(blocks[c])
        if c:
            summed, _ = lax.optimization_barrier((summed, gathered[-1][0]))
        u_own.append(masked(mask_own[c], summed, r0_own[c]))
        gathered.append(to_plane(u_own[c]))
    seconds, u = products(gathered, [u_own[1:]] + none[1:])
    got = [exchange(seconds[c]) for c in each]
    blocks = [place_blocks(got[0], seconds[-1][:1])]
    u_late, _ = lax.optimization_barrier((u_own, blocks[0]))
    scalars = total(
        [
            column_dot(r0_all, r0_all),
            jnp.concatenate([column_dot(r0_own[c], u_late[c]) for c in each]),
        ]
    )
    blocks += [place_blocks(got[c], [scalars]) for c in each[1:]]
    kept, gathered, turns = [], [], []
    for c in each:
        n0, c00 = scalars[:, cuts[c]]
        summed = home(blocks[c])
        if c:
            summed, _ = lax.optimization_barrier((summed, turns[-1]))
        uu_own = masked(mask_own[c], summed, u_own[c])
        a0 = n0 / (c00 + epsilon)
        r1_own = r0_own[c] - a0 * u_own[c]
        s1_own = u_own[c] - a0 * uu_own
        n1, c11, c01, c10 = total(
            [
                column_dot(r1_own, r1_own),
                column_dot(r1_own, s1_own),
                column_dot(r0_own[c], s1_own),
                column_dot(r1_own, u_own[c]),
            ]
        )
        b0 = n1 / (n0 + epsilon)
        curve1 = c11 + b0 * (c01 + c10) + b0 * b0 * c00
        a1 = n1 / (curve1 + epsilon)
        t1_own = s1_own + b0 * u_own[c]
        r2_own = r1_own - a1 * t1_own
        kept.append((a0, b0, a1, n1, curve1, t1_own, r2_own))
        gathered.append(to_plane(r2_own))
        turns.append(turned(r2_own))

    afters = [[turns[c]] for c in each]
    others = [turned_out(turns[c], kept[-1][-1]) for c in each]
    afters[0] = afters[0] + [k[-1] for k in kept[1:]]
    thirds, r2 = products(gathered, afters)
    parts = []
    for c in each:
        t1_own, r2_own = kept[c][-2:]
        form = form_of(thirds[c], turns[c], others[c], gathered[c][0])
        parts.append(
            [form, column_dot(r2_own, r2_own), column_dot(r2_own, t1_own)]
        )
    scalars = total([jnp.concatenate(part) for part in zip(*parts)])
    buffer = None
    for c in each:
        a0, b0, a1, n1, curve1, _, _ = kept[c]
        form, n2, cross = scalars[:, cuts[c]]
        b1 = n2 / (n1 + epsilon)
        curve2 = form + damping_value * n2 + 2.0 * b1 * cross + b1 * b1 * curve1
        a2 = n2 / (curve2 + epsilon)
        on_d1 = a1 + a2 * b1
        coef = jnp.stack([a0 + on_d1 * (1.0 + b0), -on_d1 * a0, a2])[:, None, :]
        buffer = finish(coef, right_side, mask, u[c], r2[c], c, buffer)
    return buffer


def solution(mesh):
    in_specs = (P("row", "col"), P("row", None), P("row", None), P())
    out_specs = P("row", None)

    return jax.shard_map(
        on_device, mesh=mesh, in_specs=in_specs, out_specs=out_specs, check_vma=False
    )
```

```python
import functools

import jax
import jax.numpy as jnp
from jax import lax
from jax.experimental import pallas as pl
from jax.experimental.pallas import tpu as pltpu
from jax.sharding import PartitionSpec as P


CHUNKS = 2
epsilon = 1e-06
F32, BF16 = jnp.float32, jnp.bfloat16
VMEM_LIMIT = 48 << 20


def strip_of(size):
    return next(s for s in (64, 48, 32, 16) if size % s == 0)


def split(value):
    high = value.astype(BF16)
    return high, (value - high.astype(F32)).astype(BF16)


def down(left, right):
    return lax.dot_general(
        left, right, (((0,), (0,)), ((), ())), preferred_element_type=F32
    )


def copy_strips(source, source_base, target, target_base, size):
    strip = strip_of(size)

    def body(s, carry):
        here = pl.ds(pl.multiple_of(source_base + s * strip, 16), strip)
        there = pl.ds(pl.multiple_of(target_base + s * strip, 16), strip)
        target[there, :] = source[here, :]
        return carry

    lax.fori_loop(0, size // strip, body, 0)


def product_kernel(layout, place_ref, h_ref, *refs):
    n_piece, ratio, piece, sub, low_terms, fresh, n_after = layout
    n_in = 2 if fresh else ratio
    inputs, refs = refs[:n_in], refs[n_in + n_after :]
    outputs = refs[:n_piece]
    x_out = None if fresh else refs[n_piece]
    terms, sums = refs[-2], refs[-1]
    step = pl.program_id(0)
    rows, width = h_ref.shape
    columns = sums.shape[1]
    block = n_piece * piece
    strip = strip_of(piece)

    def keep(value, at):
        high, low = split(value)
        terms[at, :columns] = high
        if low_terms:
            terms[at, columns:] = low

    @pl.when(step == 0)
    def _():
        if fresh:
            right_ref, mask_ref = inputs

            def body(s, carry):
                at = pl.ds(pl.multiple_of(s * strip, strip), strip)
                keep(mask_ref[at, :].astype(F32) * right_ref[at, :], at)
                return carry

            lax.fori_loop(0, rows // strip, body, 0)
        else:
            for j in range(ratio):
                for k in range(n_piece):
                    base = (place_ref[1] ^ j) * block + (place_ref[0] ^ k) * piece

                    def body(s, carry, j=j, k=k, base=base):
                        start = pl.multiple_of(k * piece + s * strip, strip)
                        at = pl.ds(pl.multiple_of(base + s * strip, 16), strip)
                        value = inputs[j][pl.ds(start, strip), :]
                        keep(value, at)
                        x_out[at, :] = value
                        return carry

                    lax.fori_loop(0, piece // strip, body, 0)

    summed = None
    for s in range(rows // sub):
        at = slice(s * sub, (s + 1) * sub)
        high, low = split(h_ref[at, :])
        part = down(high, terms[at, :])
        if low_terms:
            part = part[:, :columns] + part[:, columns:]
        part = part + down(low, terms[at, :columns])
        summed = part if summed is None else summed + part
    sums[pl.ds(pl.multiple_of(step * width, 128), width), :] = summed

    @pl.when(step == pl.num_programs(0) - 1)
    def _():
        for k in range(n_piece):
            copy_strips(sums, (place_ref[0] ^ k) * piece, outputs[k], 0, piece)


def product(hessian, place, inputs, columns, piece, chunk=None, after=()):
    low_terms = True
    rows, block = hessian.shape
    n_piece = block // piece
    ratio = rows // block
    fresh = chunk is not None
    width = max(w for w in (128, 256, 384) if block % w == 0 and w * rows <= 1 << 21)
    sub = min(rows, 2304)
    if rows % sub:
        sub = rows
    whole = lambda shape, at=0: pl.BlockSpec(shape, lambda i, p: (0, at))
    if fresh:
        in_specs = [whole((rows, columns), chunk)] * 2
    else:
        in_specs = [whole((block, columns))] * ratio
    out_shape = [jax.ShapeDtypeStruct((piece, columns), F32)] * n_piece
    out_specs = [whole((piece, columns))] * n_piece
    if not fresh:
        out_shape.append(jax.ShapeDtypeStruct((rows, columns), F32))
        out_specs.append(whole((rows, columns)))
    in_specs += [pl.BlockSpec(memory_space=pl.ANY)] * len(after)
    layout = (n_piece, ratio, piece, sub, low_terms, fresh, len(after))
    passes = 3 if low_terms else 2
    return pl.pallas_call(
        functools.partial(product_kernel, layout),
        out_shape=out_shape,
        grid_spec=pltpu.PrefetchScalarGridSpec(
            num_scalar_prefetch=1,
            grid=(block // width,),
            in_specs=[pl.BlockSpec((rows, width), lambda i, p: (0, i))] + in_specs,
            out_specs=out_specs,
            scratch_shapes=[
                pltpu.VMEM((rows, columns * (2 if low_terms else 1)), BF16),
                pltpu.VMEM((block, columns), F32),
            ],
        ),
        compiler_params=pltpu.CompilerParams(
            dimension_semantics=("arbitrary",), vmem_limit_bytes=VMEM_LIMIT
        ),
        cost_estimate=pl.CostEstimate(
            flops=2 * passes * rows * block * columns,
            bytes_accessed=4 * (rows * block + rows * columns + block * columns),
            transcendentals=0,
        ),
    )(place, hessian, *inputs, *after)


def assemble_kernel(count, place_ref, *refs):
    pieces, out_ref = refs[:count], refs[-1]
    size = pieces[0].shape[0]
    for k, piece in enumerate(pieces):
        copy_strips(piece, 0, out_ref, (place_ref[0] ^ k) * size, size)


def assemble(pieces, place, after=()):
    size, columns = pieces[0].shape
    return pl.pallas_call(
        functools.partial(assemble_kernel, len(pieces)),
        out_shape=jax.ShapeDtypeStruct((size * len(pieces), columns), F32),
        in_specs=[pl.BlockSpec(memory_space=pltpu.SMEM)]
        + [pl.BlockSpec(memory_space=pltpu.VMEM)] * len(pieces)
        + [pl.BlockSpec(memory_space=pl.ANY)] * len(after),
        out_specs=pl.BlockSpec(memory_space=pltpu.VMEM),
        cost_estimate=pl.CostEstimate(
            flops=0,
            bytes_accessed=8 * size * columns * len(pieces),
            transcendentals=0,
        ),
    )(place, *pieces, *after)


def turn_kernel(count, place_ref, *refs):
    groups = (len(refs) - 1) // (2 * count)
    inputs = refs[: groups * count]
    outputs = refs[-groups * count :]
    for group in range(groups):
        for j in range(count):
            for k in range(count):

                @pl.when((place_ref[0] ^ j) == k)
                def _(group=group, j=j, k=k):
                    source, target = inputs[group * count + k], outputs[group * count + j]
                    copy_strips(source, 0, target, 0, source.shape[0])


def turn(groups, place, after):
    count = len(groups[0])
    flat = [x for group in groups for x in group]
    out = pl.pallas_call(
        functools.partial(turn_kernel, count),
        out_shape=[jax.ShapeDtypeStruct(x.shape, F32) for x in flat],
        in_specs=[pl.BlockSpec(memory_space=pltpu.SMEM)]
        + [pl.BlockSpec(memory_space=pltpu.VMEM)] * len(flat)
        + [pl.BlockSpec(memory_space=pl.ANY)],
        out_specs=[pl.BlockSpec(memory_space=pltpu.VMEM)] * len(flat),
        cost_estimate=pl.CostEstimate(
            flops=0, bytes_accessed=8 * len(flat) * flat[0].size, transcendentals=0
        ),
    )(place, *flat, after)
    return [out[g * count : (g + 1) * count] for g in range(len(groups))]


def swap(block, axis, distance):
    size = lax.axis_size(axis)
    return lax.ppermute(block, axis, [(i, i ^ distance) for i in range(size)])


def total(parts):
    parts = jnp.stack(parts)
    for axis in ("col", "row"):
        distance = 1
        while distance < lax.axis_size(axis):
            parts = parts + swap(parts, axis, distance)
            distance *= 2
    return parts


def column_dot(first, second):
    return jnp.sum(first * second, axis=0)


def take(whole, place, size):
    return lax.dynamic_slice_in_dim(whole, place, size, 0)


def finish_kernel(coef_ref, right_ref, mask_ref, u_ref, r2_ref, *refs):
    strip = strip_of(u_ref.shape[0])

    def body(s, carry):
        at = pl.ds(pl.multiple_of(s * strip, strip), strip)
        r0 = mask_ref[at, :].astype(F32) * right_ref[at, :]
        value = coef_ref[0] * r0 + coef_ref[1] * u_ref[at, :] + coef_ref[2] * r2_ref[at, :]
        refs[-1][at, :] = value
        return carry

    lax.fori_loop(0, u_ref.shape[0] // strip, body, 0)


def finish(coef, right_side, mask, u, r2, chunk, buffer):
    rows, columns = u.shape
    size = rows // 8
    here = pl.BlockSpec((size, columns), lambda i: (i, chunk))
    own = pl.BlockSpec((size, columns), lambda i: (i, 0))
    given = [] if buffer is None else [buffer]
    return pl.pallas_call(
        finish_kernel,
        out_shape=jax.ShapeDtypeStruct(right_side.shape, F32),
        grid=(8,),
        in_specs=[pl.BlockSpec(coef.shape, lambda i: (0, 0, 0)), here, here, own, own]
        + [pl.BlockSpec(memory_space=pl.ANY)] * len(given),
        out_specs=here,
        input_output_aliases={5: 0} if given else {},
        cost_estimate=pl.CostEstimate(
            flops=6 * rows * columns, bytes_accessed=20 * rows * columns, transcendentals=0
        ),
    )(coef, right_side, mask, u, r2, *given)


def on_device(hessian, right_side, mask, damping):
    n_row, n_col = lax.axis_size("row"), lax.axis_size("col")
    ratio = n_col // n_row
    rows, block = hessian.shape
    piece = rows // n_col
    columns = right_side.shape[1] // CHUNKS
    damping_value = damping[0]
    col = lax.axis_index("col")
    plane, half = col // ratio, col % ratio
    level = lax.axis_index("row")
    own_place = half * block + plane * piece
    at_plane = jnp.stack([plane, half]).astype(jnp.int32)
    at_level = jnp.stack([level]).astype(jnp.int32)
    everyone = range(1, n_row)

    def exchange(pieces):
        return [pieces[0]] + [swap(pieces[k], "col", k * ratio) for k in everyone]

    def place_blocks(pieces, after):
        return assemble(pieces, at_plane, after)

    def home(blocks):
        return lax.psum_scatter(blocks, "row", scatter_dimension=0, tiled=True)

    def to_plane(shard):
        got = exchange([shard] * n_row)
        mine = assemble(got, jnp.zeros_like(at_level))
        return [mine] + [swap(mine, "col", k) for k in range(1, ratio)]

    def levels_of(shard):
        low, high = jnp.split(shard, 2, axis=1)
        got = [low]
        for k in everyone:
            got.append(swap(jnp.where((level ^ k) < level, low, high), "row", k))
        return got

    def form_of(pieces, others, mine):
        summed, own = 0.0, 0.0
        for k in range(n_row):
            low, high = jnp.split(pieces[k], 2, axis=1)
            summed += column_dot(jnp.where(plane > level, low, high), others[k])
            own += column_dot(pieces[k], mine[k * piece : (k + 1) * piece])
        zero = jnp.zeros_like(summed)
        pair = jnp.concatenate(
            [
                jnp.where(plane > level, 2.0 * summed, zero),
                jnp.where(plane < level, 2.0 * summed, zero),
            ]
        )
        return jnp.where(plane == level, own, pair)

    def masked(mask_own, summed, own):
        return mask_own * (summed + damping_value * own)

    each = range(CHUNKS)
    cuts = [slice(c * columns, (c + 1) * columns) for c in each]
    mask_all = take(mask, own_place, piece).astype(F32)
    r0_all = mask_all * take(right_side, own_place, piece)
    mask_own = [mask_all[:, cut] for cut in cuts]
    r0_own = [r0_all[:, cut] for cut in cuts]

    def products(inputs, afters, fresh=False):
        pieces, wholes = [], []
        for c in each:
            after = [*afters[c], *(pieces[-1][:1] if c else ())]
            chunk = c if fresh else None
            out = product(hessian, at_plane, inputs[c], columns, piece, chunk, after)
            pieces.append(out[:n_row])
            wholes.extend(out[n_row:])
        return pieces, wholes

    none = [[]] * CHUNKS
    firsts, _ = products([(right_side, mask)] * CHUNKS, none, True)
    got = [exchange(firsts[c]) for c in each]
    blocks = [place_blocks(got[0], firsts[-1][:1])]
    blocks += [place_blocks(got[c], blocks[:1]) for c in each[1:]]
    u_own, gathered = [], []
    for c in each:
        summed = home(blocks[c])
        if c:
            summed, _ = lax.optimization_barrier((summed, gathered[-1][0]))
        u_own.append(masked(mask_own[c], summed, r0_own[c]))
        gathered.append(to_plane(u_own[c]))
    seconds, u = products(gathered, [u_own[1:]] + none[1:])
    got = [exchange(seconds[c]) for c in each]
    blocks = [place_blocks(got[0], seconds[-1][:1])]
    u_late, _ = lax.optimization_barrier((u_own, blocks[0]))
    scalars = total(
        [
            column_dot(r0_all, r0_all),
            jnp.concatenate([column_dot(r0_own[c], u_late[c]) for c in each]),
        ]
    )
    blocks += [place_blocks(got[c], [scalars]) for c in each[1:]]

    def hold(value, *others):
        return lax.optimization_barrier((value, others))[0]

    kept, gathered = [], []
    for c in each:
        n0, c00 = scalars[:, cuts[c]]
        summed = home(blocks[c])
        if c:
            summed = hold(summed, gathered[-1][0])
        uu_own = masked(mask_own[c], summed, u_own[c])
        a0 = n0 / (c00 + epsilon)
        r1_own = r0_own[c] - a0 * u_own[c]
        s1_own = u_own[c] - a0 * uu_own
        w_own = r1_own - a0 * s1_own
        gathered.append(to_plane(w_own))
        kept.append((a0, gathered[c][0], r1_own, s1_own, w_own, uu_own))
    w_last = kept[-1][4]
    got = [levels_of(hold(kept[c][4], w_last)) for c in each]
    others, thirds, w = [], [], []
    for c in each:
        after = [w_last]
        if c:
            turned = turn(got, jnp.stack([level ^ plane]), thirds[0][0])
            others = [exchange(turned[d]) for d in each]
            after = [turned[-1][0]]
        *pieces, whole = product(
            hessian, at_plane, gathered[c], columns, piece, after=after
        )
        thirds.append(pieces)
        w.append(whole)
    rows_of = []
    for c in each:
        a0, mine, r1, s1, w_own, uu = kept[c]
        u_c = u_own[c]
        form = form_of(thirds[c], others[c], mine)
        pairs = (
            (r1, r1), (r1, s1), (r0_own[c], s1), (r1, u_c), (w_own, w_own), (w_own, r1),
            (w_own, u_c), (w_own, s1), (w_own, uu), (u_c, uu), (u_c, u_c), (u_c, s1),
        )
        rows_of.append([form] + [column_dot(*pair) for pair in pairs])
    sums = total([jnp.concatenate(part) for part in zip(*rows_of)])
    buffer = None
    for c in each:
        n0, c00 = scalars[:, cuts[c]]
        a0 = kept[c][0]
        form, n1, c11, c01, c10, ww, wr, wu, ws, wuu, uuu, u2, us = sums[:, cuts[c]]
        b0 = n1 / (n0 + epsilon)
        curve1 = c11 + b0 * (c01 + c10) + b0 * b0 * c00
        a1 = n1 / (curve1 + epsilon)
        c2 = jnp.where(a0 > 0.0, a1 / jnp.where(a0 > 0.0, a0, 1.0), 0.0)
        c1, c3 = 1.0 - c2, -a1 * b0
        n2 = c1 * c1 * n1 + c2 * c2 * ww + c3 * c3 * u2
        n2 = n2 + 2.0 * (c1 * c2 * wr + c1 * c3 * c10 + c2 * c3 * wu)
        n2 = jnp.maximum(n2, 0.0)
        cross = c1 * (c11 + b0 * c10) + c2 * (ws + b0 * wu) + c3 * (us + b0 * u2)
        curve2 = c2 * c2 * (form + damping_value * ww) + c1 * c1 * c11 + c3 * c3 * uuu
        curve2 = curve2 + 2.0 * (c1 * c2 * ws + c2 * c3 * wuu + c1 * c3 * us)
        b1 = n2 / (n1 + epsilon)
        curve2 = curve2 + 2.0 * b1 * cross + b1 * b1 * curve1
        a2 = n2 / (jnp.maximum(curve2, damping_value * n2) + epsilon)
        on_d1 = a1 + a2 * b1
        on_r1 = on_d1 + a2 * c1
        coef = jnp.stack([a0 + on_d1 * b0 + on_r1, a2 * c3 - a0 * on_r1, a2 * c2])
        buffer = finish(coef[:, None, :], right_side, mask, u[c], w[c], c, buffer)
    return buffer


def solution(mesh):
    in_specs = (P("row", "col"), P("row", None), P("row", None), P())
    out_specs = P("row", None)

    return jax.shard_map(
        on_device, mesh=mesh, in_specs=in_specs, out_specs=out_specs, check_vma=False
    )
```

```python
import functools

import jax
import jax.numpy as jnp
from jax import lax
from jax.experimental import pallas as pl
from jax.experimental.pallas import tpu as pltpu
from jax.sharding import PartitionSpec as P


CHUNKS = 2
epsilon = 1e-06
F32, BF16 = jnp.float32, jnp.bfloat16
VMEM_LIMIT = 48 << 20


def strip_of(size):
    return next(s for s in (64, 48, 32, 16) if size % s == 0)


def split(value):
    high = value.astype(BF16)
    return high, (value - high.astype(F32)).astype(BF16)


def down(left, right):
    return lax.dot_general(
        left, right, (((0,), (0,)), ((), ())), preferred_element_type=F32
    )


def copy_strips(source, source_base, target, target_base, size):
    strip = strip_of(size)

    def body(s, carry):
        here = pl.ds(pl.multiple_of(source_base + s * strip, 16), strip)
        there = pl.ds(pl.multiple_of(target_base + s * strip, 16), strip)
        target[there, :] = source[here, :]
        return carry

    lax.fori_loop(0, size // strip, body, 0)


def product_kernel(layout, place_ref, h_ref, *refs):
    n_piece, ratio, piece, sub, low_terms, fresh, n_after = layout
    n_in = 2 if fresh else ratio
    inputs, refs = refs[:n_in], refs[n_in + n_after :]
    outputs = refs[:n_piece]
    x_out = None if fresh else refs[n_piece]
    terms, sums = refs[-2], refs[-1]
    step = pl.program_id(0)
    rows, width = h_ref.shape
    columns = sums.shape[1]
    block = n_piece * piece
    strip = strip_of(piece)

    def keep(value, at):
        high, low = split(value)
        terms[at, :columns] = high
        if low_terms:
            terms[at, columns:] = low

    @pl.when(step == 0)
    def _():
        if fresh:
            right_ref, mask_ref = inputs

            def body(s, carry):
                at = pl.ds(pl.multiple_of(s * strip, strip), strip)
                keep(mask_ref[at, :].astype(F32) * right_ref[at, :], at)
                return carry

            lax.fori_loop(0, rows // strip, body, 0)
        else:
            for j in range(ratio):
                for k in range(n_piece):
                    base = (place_ref[1] ^ j) * block + (place_ref[0] ^ k) * piece

                    def body(s, carry, j=j, k=k, base=base):
                        start = pl.multiple_of(k * piece + s * strip, strip)
                        at = pl.ds(pl.multiple_of(base + s * strip, 16), strip)
                        value = inputs[j][pl.ds(start, strip), :]
                        keep(value, at)
                        x_out[at, :] = value
                        return carry

                    lax.fori_loop(0, piece // strip, body, 0)

    summed = None
    for s in range(rows // sub):
        at = slice(s * sub, (s + 1) * sub)
        high, low = split(h_ref[at, :])
        part = down(high, terms[at, :])
        if low_terms:
            part = part[:, :columns] + part[:, columns:]
        part = part + down(low, terms[at, :columns])
        summed = part if summed is None else summed + part
    sums[pl.ds(pl.multiple_of(step * width, 128), width), :] = summed

    @pl.when(step == pl.num_programs(0) - 1)
    def _():
        for k in range(n_piece):
            copy_strips(sums, (place_ref[0] ^ k) * piece, outputs[k], 0, piece)


def product(hessian, place, inputs, columns, piece, chunk=None, after=()):
    low_terms = True
    rows, block = hessian.shape
    n_piece = block // piece
    ratio = rows // block
    fresh = chunk is not None
    width = max(w for w in (128, 256, 384) if block % w == 0 and w * rows <= 1 << 21)
    sub = min(rows, 2304)
    if rows % sub:
        sub = rows
    whole = lambda shape, at=0: pl.BlockSpec(shape, lambda i, p: (0, at))
    if fresh:
        in_specs = [whole((rows, columns), chunk)] * 2
    else:
        in_specs = [whole((block, columns))] * ratio
    out_shape = [jax.ShapeDtypeStruct((piece, columns), F32)] * n_piece
    out_specs = [whole((piece, columns))] * n_piece
    if not fresh:
        out_shape.append(jax.ShapeDtypeStruct((rows, columns), F32))
        out_specs.append(whole((rows, columns)))
    in_specs += [pl.BlockSpec(memory_space=pl.ANY)] * len(after)
    layout = (n_piece, ratio, piece, sub, low_terms, fresh, len(after))
    passes = 3 if low_terms else 2
    return pl.pallas_call(
        functools.partial(product_kernel, layout),
        out_shape=out_shape,
        grid_spec=pltpu.PrefetchScalarGridSpec(
            num_scalar_prefetch=1,
            grid=(block // width,),
            in_specs=[pl.BlockSpec((rows, width), lambda i, p: (0, i))] + in_specs,
            out_specs=out_specs,
            scratch_shapes=[
                pltpu.VMEM((rows, columns * (2 if low_terms else 1)), BF16),
                pltpu.VMEM((block, columns), F32),
            ],
        ),
        compiler_params=pltpu.CompilerParams(
            dimension_semantics=("arbitrary",), vmem_limit_bytes=VMEM_LIMIT
        ),
        cost_estimate=pl.CostEstimate(
            flops=2 * passes * rows * block * columns,
            bytes_accessed=4 * (rows * block + rows * columns + block * columns),
            transcendentals=0,
        ),
    )(place, hessian, *inputs, *after)


def assemble_kernel(count, place_ref, *refs):
    pieces, out_ref = refs[:count], refs[-1]
    size = pieces[0].shape[0]
    for k, piece in enumerate(pieces):
        copy_strips(piece, 0, out_ref, (place_ref[0] ^ k) * size, size)


def assemble(pieces, place, after=()):
    size, columns = pieces[0].shape
    return pl.pallas_call(
        functools.partial(assemble_kernel, len(pieces)),
        out_shape=jax.ShapeDtypeStruct((size * len(pieces), columns), F32),
        in_specs=[pl.BlockSpec(memory_space=pltpu.SMEM)]
        + [pl.BlockSpec(memory_space=pltpu.VMEM)] * len(pieces)
        + [pl.BlockSpec(memory_space=pl.ANY)] * len(after),
        out_specs=pl.BlockSpec(memory_space=pltpu.VMEM),
        cost_estimate=pl.CostEstimate(
            flops=0,
            bytes_accessed=8 * size * columns * len(pieces),
            transcendentals=0,
        ),
    )(place, *pieces, *after)


def turn_kernel(count, place_ref, *refs):
    groups = (len(refs) - 1) // (2 * count)
    inputs = refs[: groups * count]
    outputs = refs[-groups * count :]
    for group in range(groups):
        for j in range(count):
            for k in range(count):

                @pl.when((place_ref[0] ^ j) == k)
                def _(group=group, j=j, k=k):
                    source, target = inputs[group * count + k], outputs[group * count + j]
                    copy_strips(source, 0, target, 0, source.shape[0])


def turn(groups, place, after):
    count = len(groups[0])
    flat = [x for group in groups for x in group]
    out = pl.pallas_call(
        functools.partial(turn_kernel, count),
        out_shape=[jax.ShapeDtypeStruct(x.shape, F32) for x in flat],
        in_specs=[pl.BlockSpec(memory_space=pltpu.SMEM)]
        + [pl.BlockSpec(memory_space=pltpu.VMEM)] * len(flat)
        + [pl.BlockSpec(memory_space=pl.ANY)],
        out_specs=[pl.BlockSpec(memory_space=pltpu.VMEM)] * len(flat),
        cost_estimate=pl.CostEstimate(
            flops=0, bytes_accessed=8 * len(flat) * flat[0].size, transcendentals=0
        ),
    )(place, *flat, after)
    return [out[g * count : (g + 1) * count] for g in range(len(groups))]


def swap(block, axis, distance):
    size = lax.axis_size(axis)
    return lax.ppermute(block, axis, [(i, i ^ distance) for i in range(size)])


def total(parts):
    for axis in ("col", "row"):
        distance = 1
        while distance < lax.axis_size(axis):
            parts = parts + swap(parts, axis, distance)
            distance *= 2
    return parts


def column_dot(first, second):
    return jnp.sum(first * second, axis=0)


def take(whole, place, size):
    return lax.dynamic_slice_in_dim(whole, place, size, 0)


def finish_kernel(coef_ref, right_ref, mask_ref, u_ref, r2_ref, *refs):
    strip = strip_of(u_ref.shape[0])

    def body(s, carry):
        at = pl.ds(pl.multiple_of(s * strip, strip), strip)
        r0 = mask_ref[at, :].astype(F32) * right_ref[at, :]
        value = coef_ref[0] * r0 + coef_ref[1] * u_ref[at, :] + coef_ref[2] * r2_ref[at, :]
        refs[-1][at, :] = value
        return carry

    lax.fori_loop(0, u_ref.shape[0] // strip, body, 0)


def finish(coef, right_side, mask, u, r2, chunk, buffer):
    rows, columns = u.shape
    size = rows // 8
    here = pl.BlockSpec((size, columns), lambda i: (i, chunk))
    own = pl.BlockSpec((size, columns), lambda i: (i, 0))
    given = [] if buffer is None else [buffer]
    return pl.pallas_call(
        finish_kernel,
        out_shape=jax.ShapeDtypeStruct(right_side.shape, F32),
        grid=(8,),
        in_specs=[pl.BlockSpec(coef.shape, lambda i: (0, 0, 0)), here, here, own, own]
        + [pl.BlockSpec(memory_space=pl.ANY)] * len(given),
        out_specs=here,
        input_output_aliases={5: 0} if given else {},
        cost_estimate=pl.CostEstimate(
            flops=6 * rows * columns, bytes_accessed=20 * rows * columns, transcendentals=0
        ),
    )(coef, right_side, mask, u, r2, *given)


def on_device(hessian, right_side, mask, damping):
    n_row, n_col = lax.axis_size("row"), lax.axis_size("col")
    ratio = n_col // n_row
    rows, block = hessian.shape
    piece = rows // n_col
    columns = right_side.shape[1] // CHUNKS
    damping_value = damping[0]
    col = lax.axis_index("col")
    plane, half = col // ratio, col % ratio
    level = lax.axis_index("row")
    own_place = half * block + plane * piece
    at_plane = jnp.stack([plane, half]).astype(jnp.int32)
    at_level = jnp.stack([level]).astype(jnp.int32)
    everyone = range(1, n_row)

    def exchange(pieces):
        return [pieces[0]] + [swap(pieces[k], "col", k * ratio) for k in everyone]

    def place_blocks(pieces, after):
        return assemble(pieces, at_plane, after)

    def home(blocks):
        return lax.psum_scatter(blocks, "row", scatter_dimension=0, tiled=True)

    def to_plane(shard):
        got = exchange([shard] * n_row)
        mine = assemble(got, jnp.zeros_like(at_level))
        return [mine] + [swap(mine, "col", k) for k in range(1, ratio)]

    def levels_of(shard):
        low, high = jnp.split(shard, 2, axis=1)
        got = [low]
        for k in everyone:
            got.append(swap(jnp.where((level ^ k) < level, low, high), "row", k))
        return got

    def form_of(pieces, others, mine):
        summed, own = 0.0, 0.0
        for k in range(n_row):
            low, high = jnp.split(pieces[k], 2, axis=1)
            summed += column_dot(jnp.where(plane > level, low, high), others[k])
            own += column_dot(pieces[k], mine[k * piece : (k + 1) * piece])
        zero = jnp.zeros_like(summed)
        pair = jnp.concatenate(
            [
                jnp.where(plane > level, 2.0 * summed, zero),
                jnp.where(plane < level, 2.0 * summed, zero),
            ]
        )
        return jnp.where(plane == level, own, pair)

    def masked(mask_own, summed, own):
        return mask_own * (summed + damping_value * own)

    each = range(CHUNKS)
    cuts = [slice(c * columns, (c + 1) * columns) for c in each]
    mask_all = take(mask, own_place, piece).astype(F32)
    r0_all = mask_all * take(right_side, own_place, piece)
    mask_own = [mask_all[:, cut] for cut in cuts]
    r0_own = [r0_all[:, cut] for cut in cuts]

    def products(inputs, afters, fresh=False):
        pieces, wholes = [], []
        for c in each:
            after = [*afters[c], *(pieces[-1][:1] if c else ())]
            chunk = c if fresh else None
            out = product(hessian, at_plane, inputs[c], columns, piece, chunk, after)
            pieces.append(out[:n_row])
            wholes.extend(out[n_row:])
        return pieces, wholes

    none = [[]] * CHUNKS
    firsts, _ = products([(right_side, mask)] * CHUNKS, none, True)
    got = [exchange(firsts[c]) for c in each]
    blocks = [place_blocks(got[0], firsts[-1][:1])]
    blocks += [place_blocks(got[c], blocks[:1]) for c in each[1:]]
    u_own, gathered = [], []
    for c in each:
        summed = home(blocks[c])
        if c:
            summed, _ = lax.optimization_barrier((summed, gathered[-1][0]))
        u_own.append(masked(mask_own[c], summed, r0_own[c]))
        gathered.append(to_plane(u_own[c]))
    seconds, u = products(gathered, [u_own[1:]] + none[1:])
    got = [exchange(seconds[c]) for c in each]
    blocks = [place_blocks(got[0], seconds[-1][:1])]
    u_late, _ = lax.optimization_barrier((u_own, blocks[0]))
    over_u = jnp.concatenate([column_dot(r0_own[c], u_late[c]) for c in each])
    scalars = total(jnp.stack([column_dot(r0_all, r0_all), over_u]))
    blocks += [place_blocks(got[c], [scalars]) for c in each[1:]]

    def hold(value, *others):
        return lax.optimization_barrier((value, others))[0]

    kept, gathered, dots = [], [], []
    for c in each:
        n0, c00 = scalars[:, cuts[c]]
        summed = home(blocks[c])
        if c:
            summed = hold(summed, gathered[-1][0], dots[-1])
        uu_own = masked(mask_own[c], summed, u_own[c])
        a0 = n0 / (c00 + epsilon)
        r1_own = r0_own[c] - a0 * u_own[c]
        s1_own = u_own[c] - a0 * uu_own
        w_own = r1_own - a0 * s1_own
        gathered.append(to_plane(w_own))
        kept.append((a0, gathered[c][0], w_own))
        u_c = u_own[c]
        pairs = (
            (r1_own, r1_own),
            (r1_own, s1_own),
            (r0_own[c], s1_own),
            (r1_own, u_c),
            (w_own, w_own),
            (w_own, r1_own),
            (w_own, u_c),
            (w_own, s1_own),
            (w_own, uu_own),
            (u_c, uu_own),
            (u_c, u_c),
            (u_c, s1_own),
        )
        dots.append(jnp.stack([column_dot(*pair) for pair in pairs]))
    w_last = kept[-1][2]
    got = [levels_of(hold(kept[c][2], summed if c < 1 else w_last)) for c in each]
    others, thirds, w = [], [], []
    for c in each:
        after = [w_last]
        if c:
            turned = turn(got, jnp.stack([level ^ plane]), thirds[0][0])
            others = [exchange(turned[d]) for d in each]
            after = [turned[-1][0]]
        *pieces, whole = product(
            hessian, at_plane, gathered[c], columns, piece, after=after
        )
        thirds.append(pieces)
        w.append(whole)
    forms = [form_of(thirds[c], others[c], kept[c][1])[None] for c in each]
    rows_of = [jnp.concatenate(part) for part in zip(forms, dots)]
    sums = total(jnp.concatenate(rows_of, axis=1))
    buffer = None
    for c in each:
        n0, c00 = scalars[:, cuts[c]]
        a0 = kept[c][0]
        form, n1, c11, c01, c10, ww, wr, wu, ws, wuu, uuu, u2, us = sums[:, cuts[c]]
        b0 = n1 / (n0 + epsilon)
        curve1 = c11 + b0 * (c01 + c10) + b0 * b0 * c00
        a1 = n1 / (curve1 + epsilon)
        c2 = jnp.where(a0 > 0.0, a1 / jnp.where(a0 > 0.0, a0, 1.0), 0.0)
        c1, c3 = 1.0 - c2, -a1 * b0
        n2 = c1 * c1 * n1 + c2 * c2 * ww + c3 * c3 * u2
        n2 = n2 + 2.0 * (c1 * c2 * wr + c1 * c3 * c10 + c2 * c3 * wu)
        n2 = jnp.maximum(n2, 0.0)
        cross = c1 * (c11 + b0 * c10) + c2 * (ws + b0 * wu) + c3 * (us + b0 * u2)
        curve2 = c2 * c2 * (form + damping_value * ww) + c1 * c1 * c11 + c3 * c3 * uuu
        curve2 = curve2 + 2.0 * (c1 * c2 * ws + c2 * c3 * wuu + c1 * c3 * us)
        b1 = n2 / (n1 + epsilon)
        curve2 = curve2 + 2.0 * b1 * cross + b1 * b1 * curve1
        a2 = n2 / (jnp.maximum(curve2, damping_value * n2) + epsilon)
        on_d1 = a1 + a2 * b1
        on_r1 = on_d1 + a2 * c1
        coef = jnp.stack([a0 + on_d1 * b0 + on_r1, a2 * c3 - a0 * on_r1, a2 * c2])
        buffer = finish(coef[:, None, :], right_side, mask, u[c], w[c], c, buffer)
    return buffer


def solution(mesh):
    in_specs = (P("row", "col"), P("row", None), P("row", None), P())
    out_specs = P("row", None)

    return jax.shard_map(
        on_device, mesh=mesh, in_specs=in_specs, out_specs=out_specs, check_vma=False
    )
```
